256 devices in a mesh: dp: 32 (over y, x, core), tensor: 8 (over z).
Axes of the slice: x: 4, y: 4, z: 8, core: 2. Of those that a mesh axis runs over, the one named last changes fastest.
Arguments:
- hidden: bfloat16 [16384, 4096], P('dp', 'tensor')
- w_query: bfloat16 [4096, 4096], P(None, 'tensor')
- w_key: bfloat16 [4096, 1024], P(None, 'tensor')
- w_value: bfloat16 [4096, 1024], P(None, 'tensor'), may hold values from -0.09375 to 0.09375
- w_out: bfloat16 [4096, 4096], P('tensor'), may hold values from -0.09375 to 0.09375
- doc_ids: int32 [16384], P('dp'), may hold values from 0 to 16383, as said below
- send_counts: int32 [32, 32], replicated, may hold values from 0 to 16, as said below
Outputs:
- attended: bfloat16 [32768, 4096], P('dp', 'tensor')
The draws below stay inside these ranges and needn't reach their ends.
Inputs may be any that keep to these rules, and one draw needn't show every extreme that they name: `send_counts`: the diagonal is zero and each row sums to less than 512. On index i of dp the rows that stay come first, then the rows for each destination j in increasing order of j, each such block one whole document. `doc_ids`: the rows of one document lie together on one index of dp and share one id; different documents have different ids.
All inputs are finite; a program needn't handle non-finite values.
Results may differ from the reference program's by a relative error of at most 0.014.
Values may be sent and summed in bfloat16 or wider, within the bound.
No kernel may reach another device: no remote copies, remote signals or barrier semaphores. Data moves between devices by JAX's collectives and lax.ppermute only.
A program may use at most 128 MiB of HBM per device.

```python
import jax
import jax.numpy as jnp
from jax import lax

D = 4096
HEADS = 32
KV = 8
HD = 128
TOK_DEV = 512
SLOT = 16
TOKENS = 16384
BUF = 1024
OUT_ROWS = 32768
N_DP = 32
N_TENSOR = 8


def move_plan(key):
    count_key = jax.random.fold_in(key, 11)
    coin_key = jax.random.fold_in(key, 12)
    heavy_key = jax.random.fold_in(key, 13)
    counts = jax.random.randint(count_key, (N_DP, N_DP), 0, SLOT + 1).astype(jnp.int32)
    heavy = jax.random.randint(heavy_key, (), 0, N_DP).astype(jnp.int32)
    row_index = jnp.arange(N_DP, dtype=jnp.int32)[:, None]
    col_index = jnp.arange(N_DP, dtype=jnp.int32)[None, :]
    counts = jnp.where(col_index == heavy, SLOT, counts)
    counts = jnp.where(row_index == heavy, 0, counts)
    counts = jnp.where(row_index == col_index, 0, counts)
    counts = jnp.where(col_index == (row_index + 1) % N_DP, SLOT, counts).astype(jnp.int32)
    home_len = TOK_DEV - jnp.sum(counts, axis=1)
    starts = home_len[:, None] + jnp.cumsum(counts, axis=1) - counts
    positions = jnp.arange(TOK_DEV, dtype=jnp.int32)[None, :]
    coins = jax.random.randint(coin_key, (N_DP, TOK_DEV), 0, 64)
    home_flag = (positions < home_len[:, None]) & ((coins == 0) | (positions == 0))
    block_flag = jnp.any((positions[:, :, None] == starts[:, None, :]) & (counts[:, None, :] > 0), axis=2)
    flags = home_flag | block_flag
    end_flag = jnp.concatenate([flags[:, 1:], jnp.ones((N_DP, 1), dtype=bool)], axis=1)
    positions_full = jnp.broadcast_to(positions, (N_DP, TOK_DEV))
    last = lax.cummin(jnp.where(end_flag, positions_full, TOK_DEV), axis=1, reverse=True)
    ids = jnp.arange(N_DP, dtype=jnp.int32)[:, None] * TOK_DEV + last
    return (counts, ids.reshape(-1).astype(jnp.int32))


def draw_send_counts(key, part):
    return move_plan(key)[0]


def draw_doc_ids(key, part):
    return move_plan(key)[1]


def query_base(key):
    return jax.random.normal(jax.random.fold_in(key, 21), (D, HEADS * HD), jnp.float32) * D ** (-0.5)


def draw_w_query(key, part):
    return query_base(key).astype(jnp.bfloat16)


def draw_w_key(key, part):
    fresh = jax.random.normal(jax.random.fold_in(key, 22), (D, KV * HD), jnp.float32) * D ** (-0.5)
    return fresh.astype(jnp.bfloat16)


def draw_hidden(key, part):
    values = jnp.clip(jax.random.normal(jax.random.fold_in(key, 31), (TOKENS, D), jnp.float32), -6.0, 6.0)
    return values.astype(jnp.bfloat16)


def block_levels(stream_key, dims, split, least, largest):
    level, own = 1.0, jax.random.fold_in(stream_key, 6)
    for axis_at, shards_of in split:
        heights = jnp.exp(jax.random.uniform(jax.random.fold_in(own, axis_at), (shards_of,), jnp.float32, least / len(split), largest / len(split)))
        level = level * jnp.repeat(heights, dims[axis_at] // shards_of).reshape([-1 if axis == axis_at else 1 for axis in range(len(dims))])
    return level


def gaussian(own_key, dims, width, limit, shards=(), held_as=jnp.bfloat16):
    level = block_levels(own_key, dims, shards, -0.22, 0.18) if shards else 1.0
    entries = jax.random.normal(own_key, dims, jnp.float32) * width * level
    return jnp.minimum(jnp.maximum(entries, -limit), limit).astype(held_as)


def setup_inputs(seed: int = 0) -> dict:
    splits = jax.random.split(jax.random.key(seed), 8)
    return {
        "hidden": draw_hidden(jax.random.fold_in(splits[7], 71), 0),
        "w_query": draw_w_query(jax.random.fold_in(splits[7], 71), 0),
        "w_key": draw_w_key(jax.random.fold_in(splits[7], 71), 0),
        "w_value": gaussian(splits[3], (D, KV * HD), D ** -0.5, 0.09375, ((1, 8),)),
        "w_out": gaussian(splits[4], (HEADS * HD, D), (HEADS * HD) ** -0.5, 0.09375, ((0, 8),)),
        "doc_ids": draw_doc_ids(jax.random.fold_in(splits[7], 71), 0),
        "send_counts": draw_send_counts(jax.random.fold_in(splits[7], 71), 0),
    }


def reference(hidden, w_query, w_key, w_value, w_out, doc_ids, send_counts):
    all_query = jnp.dot(hidden, w_query, preferred_element_type=jnp.float32).astype(jnp.bfloat16)
    all_key = jnp.dot(hidden, w_key, preferred_element_type=jnp.float32).astype(jnp.bfloat16)
    all_value = jnp.dot(hidden, w_value, preferred_element_type=jnp.float32).astype(jnp.bfloat16)
    home_len = TOK_DEV - jnp.sum(send_counts, axis=1)
    block_start = home_len[:, None] + jnp.cumsum(send_counts, axis=1) - send_counts
    slot_ids = jnp.arange(SLOT, dtype=jnp.int32)
    peer_ids = jnp.arange(N_DP, dtype=jnp.int32)
    out_weight = w_out.astype(jnp.float32).reshape(N_TENSOR, (HEADS * HD) // N_TENSOR, D)
    group = HEADS // KV

    def one_buffer(target):
        incoming = send_counts[:, target]
        starts = block_start[:, target]
        home_rows = (target * TOK_DEV + jnp.arange(TOK_DEV, dtype=jnp.int32)).astype(jnp.int32)
        local_rows = jnp.minimum(starts[:, None] + slot_ids[None, :], TOK_DEV - 1)
        recv_rows = (peer_ids[:, None] * TOK_DEV + local_rows).astype(jnp.int32)
        recv_valid = slot_ids[None, :] < incoming[:, None]
        index = jnp.concatenate([home_rows, recv_rows.reshape(-1)]).astype(jnp.int32)
        recv_labels = jnp.where(recv_valid, -1 - peer_ids[:, None], -1 - N_DP - peer_ids[:, None] * SLOT - slot_ids[None, :])
        labels = jnp.concatenate([doc_ids[home_rows], recv_labels.reshape(-1).astype(jnp.int32)])
        valid = jnp.concatenate([jnp.arange(TOK_DEV) < home_len[target], recv_valid.reshape(-1)])
        queries = all_query[index].astype(jnp.float32).reshape(BUF, KV, group, HD)
        key_rows = all_key[index].astype(jnp.float32).reshape(BUF, KV, HD)
        value_rows = all_value[index].astype(jnp.float32).reshape(BUF, KV, HD)
        positions = jnp.arange(BUF)
        allowed = (labels[:, None] == labels[None, :]) & (positions[None, :] <= positions[:, None])
        scores = jnp.einsum("qhgd,khd->hgqk", queries, key_rows) * (HD ** -0.5)
        scores = jnp.where(allowed[None, None], scores, -jnp.inf)
        top = jnp.max(scores, axis=-1, keepdims=True)
        expo = jnp.exp(scores - top)
        total = jnp.sum(expo, axis=-1)
        weights = lax.optimization_barrier(expo.astype(jnp.bfloat16)).astype(jnp.float32)
        mixed = jnp.einsum("hgqk,khd->qhgd", weights, value_rows) / jnp.transpose(total, (2, 0, 1))[..., None]
        mixed = lax.optimization_barrier(mixed.reshape(BUF, HEADS * HD).astype(jnp.bfloat16)).astype(jnp.float32)
        partial_sum = jnp.einsum("btc,tcd->tbd", mixed.reshape(BUF, N_TENSOR, -1), out_weight)
        partial_sum = jnp.where(valid[None, :, None], partial_sum, 0.0)
        rounded = lax.optimization_barrier(partial_sum.astype(jnp.bfloat16)).astype(jnp.float32)
        return jnp.sum(rounded, axis=0).astype(jnp.bfloat16)

    result = lax.map(one_buffer, jnp.arange(N_DP, dtype=jnp.int32))
    return result.reshape(OUT_ROWS, D)
```

```python
import jax
import jax.numpy as jnp
from jax import lax
from jax.sharding import PartitionSpec as P

HD = 128
SLOT = 16


def attend(queries, keys, values, allowed):
    count = queries.shape[0]
    kv_heads = keys.shape[1] // HD
    group = queries.shape[1] // keys.shape[1]
    query_part = queries.reshape(count, kv_heads, group, HD)
    key_part = keys.reshape(count, kv_heads, HD)
    value_part = values.reshape(count, kv_heads, HD)
    scores = jnp.einsum(
        "qhgd,khd->hgqk", query_part, key_part, preferred_element_type=jnp.float32
    ) * HD ** (-0.5)
    scores = jnp.where(allowed[None, None], scores, -jnp.inf)
    top = jnp.max(scores, axis=-1, keepdims=True)
    expo = jnp.exp(scores - top)
    total = jnp.sum(expo, axis=-1)
    mixed = jnp.einsum(
        "hgqk,khd->qhgd",
        expo.astype(jnp.bfloat16),
        value_part,
        preferred_element_type=jnp.float32,
    )
    mixed = mixed / jnp.transpose(total, (2, 0, 1))[..., None]
    return mixed.reshape(count, -1).astype(jnp.bfloat16)


def on_device(hidden, w_query, w_key, w_value, w_out, doc_ids, send_counts):
    peers = lax.axis_size("dp")
    me = lax.axis_index("dp")
    rows = hidden.shape[0]
    pos = jnp.arange(rows, dtype=jnp.int32)

    outgoing = lax.dynamic_slice_in_dim(send_counts, me, 1, 0)[0]
    home_len = rows - jnp.sum(outgoing)
    block_start = home_len + jnp.cumsum(outgoing) - outgoing
    slot_ids = jnp.arange(SLOT, dtype=jnp.int32)
    send_row = block_start[:, None] + slot_ids[None, :]
    send_row = jnp.where(slot_ids[None, :] < outgoing[:, None], send_row, -1)
    pick = (send_row.reshape(-1)[:, None] == pos[None, :]).astype(jnp.bfloat16)

    full = lax.all_gather(hidden, "tensor", axis=1, tiled=True)
    query, key, value = (
        jnp.dot(full, weight, preferred_element_type=jnp.float32).astype(jnp.bfloat16)
        for weight in (w_query, w_key, w_value)
    )
    allowed = (doc_ids[:, None] == doc_ids[None, :]) & (pos[None, :] <= pos[:, None])
    mixed = attend(query, key, value, allowed)
    partial_sum = jnp.dot(mixed, w_out, preferred_element_type=jnp.float32).astype(jnp.bfloat16)
    done = lax.psum_scatter(partial_sum, "tensor", scatter_dimension=1, tiled=True)

    home = jnp.where((pos < home_len)[:, None], done, jnp.zeros((), done.dtype))
    leaving = jnp.dot(pick, done, preferred_element_type=jnp.float32).astype(done.dtype)
    leaving = leaving.reshape(peers, SLOT, -1)
    arrived = lax.all_to_all(leaving, "dp", split_axis=0, concat_axis=0, tiled=True)
    return jnp.concatenate([home, arrived.reshape(peers * SLOT, -1)], axis=0)


def solution(mesh):
    in_specs = (
        P("dp", "tensor"),
        P(None, "tensor"),
        P(None, "tensor"),
        P(None, "tensor"),
        P("tensor", None),
        P("dp"),
        P(),
    )
    return jax.shard_map(
        on_device, mesh=mesh, in_specs=in_specs, out_specs=P("dp", "tensor"), check_vma=False
    )
```

```python
import functools

import jax
import jax.numpy as jnp
from jax import lax
from jax.experimental import pallas as pl
from jax.experimental.pallas import tpu as pltpu
from jax.sharding import PartitionSpec as P


HD = 128
SLOT = 16
BF = jnp.bfloat16
F32 = jnp.float32
SPLIT = 8
VMEM_LIMIT = 14 * 1024 * 1024


def ring_offsets(n_ring):
    offsets = [0]
    for s in range(1, n_ring // 2):
        offsets += [-s, s]
    return offsets + [n_ring // 2]


def block_start(offset, n_ring, width):
    me = lax.axis_index("tensor")
    return pl.multiple_of(lax.rem(me + (offset + n_ring), n_ring) * width, width)


def project_in(shards, wq, wk, wv, x):
    n_ring = len(shards)
    width = shards[0].shape[1]
    for shard, off in zip(shards, ring_offsets(n_ring)):
        x[:, pl.ds(block_start(off, n_ring, width), width)] = shard[...]
    rows = x[...]
    return tuple(
        jnp.dot(rows, w[...], preferred_element_type=F32).astype(BF) for w in (wq, wk, wv)
    )


def attend(query, key, value, ids, base):
    rows, keys = query.shape[0], key.shape[0]
    row = lax.broadcasted_iota(jnp.int32, (rows, keys), 0) + base
    col = lax.broadcasted_iota(jnp.int32, (rows, keys), 1)
    across = jnp.broadcast_to(ids[...], (HD, ids.shape[1]))
    down = jnp.transpose(across)[base : base + rows, :1]
    allowed = (down == ids[:, :keys]) & (col <= row)
    heads = []
    for h in range(query.shape[1] // HD):
        scores = lax.dot_general(
            query[:, h * HD : (h + 1) * HD],
            key,
            (((1,), (1,)), ((), ())),
            preferred_element_type=F32,
        ) * (HD ** -0.5)
        scores = jnp.where(allowed, scores, -jnp.inf)
        expo = jnp.exp(scores - jnp.max(scores, axis=-1, keepdims=True))
        total = jnp.sum(expo, axis=-1, keepdims=True)
        head = jnp.dot(expo.astype(BF), value, preferred_element_type=F32)
        heads.append((head / total).astype(BF))
    return jnp.concatenate(heads, axis=1)


def project_out(mixed, wo, offsets, n_ring, outs):
    width = wo.shape[1] // n_ring
    for out, off in zip(outs, offsets):
        block = wo[:, pl.ds(block_start(off, n_ring, width), width)]
        out[...] = jnp.dot(mixed, block, preferred_element_type=F32).astype(BF)


def first_kernel(n_ring, offsets, base, *refs):
    shards = refs[:n_ring]
    wq, wk, wv, wo, ids, mixed_out, k_out, v_out, *outs, x = refs[n_ring:]
    query, key, value = project_in(shards, wq, wk, wv, x)
    k_out[...] = key
    v_out[...] = value
    mixed = attend(query, key, value, ids, base)
    mixed_out[...] = mixed
    project_out(mixed, wo, offsets, n_ring, outs)


def qkv_kernel(n_ring, offsets, base, *refs):
    shards = refs[:n_ring]
    wq, wk, wv, q_out, k_out, v_out, x = refs[n_ring:]
    q_out[...], k_out[...], v_out[...] = project_in(shards, wq, wk, wv, x)


def attend_kernel(n_ring, offsets, base, q, k0, v0, k1, v1, wo, ids, mixed_out, *outs):
    key = jnp.concatenate([k0[...], k1[...]], axis=0)
    value = jnp.concatenate([v0[...], v1[...]], axis=0)
    mixed = attend(q[...], key, value, ids, base)
    mixed_out[...] = mixed
    project_out(mixed, wo, offsets, n_ring, outs)


def rest_kernel(n_ring, offsets, base, mixed, wo, *outs):
    project_out(mixed[...], wo, offsets, n_ring, outs)


def plan_kernel(counts, pick):
    peers = counts.shape[1]
    rows = pick.shape[1]
    me = lax.axis_index("dp")
    start = rows - lax.fori_loop(0, peers, lambda j, n: n + counts[me, j], 0)
    slot = lax.broadcasted_iota(jnp.int32, (SLOT, rows), 0)
    gap = lax.broadcasted_iota(jnp.int32, (SLOT, rows), 1) - slot

    def step(j, start):
        count = counts[me, j]
        hit = (gap == start) & (slot < count)
        at = pl.multiple_of(j * SLOT, SLOT)
        pick[pl.ds(at, SLOT), :] = hit.astype(F32).astype(BF)
        return start + count

    lax.fori_loop(0, peers, step, start)


def touch_kernel(*refs):
    refs[-1][...] = jnp.zeros(refs[-1].shape, BF)


def finish_kernel(counts, pick, own_a, up_a, down_a, own_b, up_b, down_b, *refs):
    *_, leaving, home = refs
    total_a = own_a[...].astype(F32) + up_a[...].astype(F32) + down_a[...].astype(F32)
    total_b = own_b[...].astype(F32) + up_b[...].astype(F32) + down_b[...].astype(F32)
    done = jnp.concatenate([total_a, total_b], axis=0)
    leaving[...] = jnp.dot(pick[...], done.astype(BF), preferred_element_type=F32).astype(BF)
    rows = done.shape[0]
    me = lax.axis_index("dp")
    kept = rows - lax.fori_loop(0, counts.shape[1], lambda j, n: n + counts[me, j], 0)
    row = lax.broadcasted_iota(jnp.int32, done.shape, 0)
    home[...] = jnp.where(row < kept, done, 0.0).astype(BF)


def call(kernel, operands, outs, scratch=(), scalars=0):
    vmem = pl.BlockSpec(memory_space=pltpu.VMEM)
    smem = pl.BlockSpec(memory_space=pltpu.SMEM)
    return pl.pallas_call(
        kernel,
        out_shape=[jax.ShapeDtypeStruct(shape, BF) for shape in outs],
        in_specs=[smem] * scalars + [vmem] * (len(operands) - scalars),
        out_specs=[vmem] * len(outs),
        scratch_shapes=scratch,
        compiler_params=pltpu.CompilerParams(vmem_limit_bytes=VMEM_LIMIT),
    )(*operands)


def on_device(hidden, w_query, w_key, w_value, w_out, doc_ids, send_counts):
    peers = lax.axis_size("dp")
    n_ring = lax.axis_size("tensor")
    rows, width = hidden.shape
    kv = w_key.shape[1]
    cut = rows * SPLIT // 16
    up = [(i, (i + 1) % n_ring) for i in range(n_ring)]
    down = [(i, (i - 1) % n_ring) for i in range(n_ring)]

    def send(x, go_up):
        return lax.ppermute(x, "tensor", up if go_up else down)

    def gather(block, far_up):
        shards, a, b = [block], block, block
        for _ in range(n_ring // 2 - 1):
            a, b = send(a, True), send(b, False)
            shards += [a, b]
        return shards + [send(a if far_up else b, far_up)]

    def add(x, y):
        return (x.astype(F32) + y.astype(F32)).astype(BF)

    def reduce(parts, far_up):
        a = send(parts[0], far_up)
        b = None
        for s in range(n_ring // 2 - 1):
            to_up, to_down = parts[1 + 2 * s], parts[2 + 2 * s]
            if s == 0:
                if far_up:
                    a, b = add(to_up, a), to_down
                else:
                    a, b = to_up, add(to_down, a)
            else:
                a, b = add(to_up, a), add(to_down, b)
            a, b = send(a, True), send(b, False)
        return parts[-1], a, b

    w_in = (w_query, w_key, w_value)
    ids = doc_ids[None, :]
    (pick,) = call(plan_kernel, (send_counts,), [(peers * SLOT, rows)], scalars=1)
    (mark_out,) = call(touch_kernel, (w_out, w_query), [(SLOT, HD)])
    (mark_in,) = call(touch_kernel, (w_key, w_value), [(SLOT, HD)])
    shards_a = gather(hidden[:cut], True)
    shards_b = gather(hidden[cut:], False)
    order = ring_offsets(n_ring)[::-1]
    tile_a, tile_b, kv_a, kv_b = (cut, width), (rows - cut, width), (cut, kv), (rows - cut, kv)
    lead_a, lead_b = (order[0], order[2]), (order[0], order[1])
    late_a = tuple(o for o in order if o not in lead_a)
    late_b = tuple(o for o in order if o not in lead_b)

    def body(kernel, offsets=(), base=0):
        return functools.partial(kernel, n_ring, offsets, base)

    mixed_a, key_a, value_a, *first_a = call(
        body(first_kernel, lead_a), (*shards_a, *w_in, w_out, ids),
        [tile_a, kv_a, kv_a, tile_a, tile_a], [pltpu.VMEM((cut, n_ring * width), BF)],
    )
    rest_a = call(body(rest_kernel, late_a), (mixed_a, w_out), [tile_a] * len(late_a))
    query_b, key_b, value_b = call(
        body(qkv_kernel), (*shards_b, *w_in), [tile_b, kv_b, kv_b],
        [pltpu.VMEM((rows - cut, n_ring * width), BF)],
    )
    mixed_b, *first_b = call(
        body(attend_kernel, lead_b, cut),
        (query_b, key_a, value_a, key_b, value_b, w_out, ids), [tile_b] * 3,
    )
    rest_b = call(body(rest_kernel, late_b), (mixed_b, w_out), [tile_b] * len(late_b))
    parts_a = dict(zip(lead_a + late_a, [*first_a, *rest_a]))
    parts_b = dict(zip(lead_b + late_b, [*first_b, *rest_b]))
    sums_a = reduce([parts_a[o] for o in order], True)
    sums_b = reduce([parts_b[o] for o in order], False)
    leaving, home = call(
        finish_kernel, (send_counts, pick, *sums_a, *sums_b, mark_out, mark_in),
        [(peers * SLOT, width), (rows, width)], scalars=1,
    )
    leaving = leaving.reshape(peers, SLOT, width)
    arrived = lax.all_to_all(leaving, "dp", split_axis=0, concat_axis=0, tiled=True)
    return jnp.concatenate([home, arrived.reshape(peers * SLOT, width)], axis=0)


def solution(mesh):
    in_specs = (
        P("dp", "tensor"),
        P(None, "tensor"),
        P(None, "tensor"),
        P(None, "tensor"),
        P("tensor", None),
        P("dp"),
        P(),
    )
    return jax.shard_map(
        on_device, mesh=mesh, in_specs=in_specs, out_specs=P("dp", "tensor"), check_vma=False
    )
```

```python
import functools

import jax
import jax.numpy as jnp
from jax import lax
from jax.experimental import pallas as pl
from jax.experimental.pallas import tpu as pltpu
from jax.sharding import PartitionSpec as P


HD = 128
SLOT = 16
BF = jnp.bfloat16
F32 = jnp.float32
SPLIT = 8
VMEM_LIMIT = 14 * 1024 * 1024


def ring_offsets(n_ring):
    offsets = [0]
    for s in range(1, n_ring // 2):
        offsets += [-s, s]
    return offsets + [n_ring // 2]


def block_start(offset, n_ring, width):
    me = lax.axis_index("tensor")
    return pl.multiple_of(lax.rem(me + (offset + n_ring), n_ring) * width, width)


def early_kernel(n_ring, wq, wk, wv, *refs):
    shards = refs[: n_ring - 1]
    q, k, v, x = refs[n_ring - 1 :]
    width = shards[0].shape[1]
    *near, far = ring_offsets(n_ring)
    x[:, pl.ds(block_start(far, n_ring, width), width)] = jnp.zeros(shards[0].shape, BF)
    for shard, off in zip(shards, near):
        x[:, pl.ds(block_start(off, n_ring, width), width)] = shard[...]
    rows = x[...]
    for out, w in zip((q, k, v), (wq, wk, wv)):
        out[...] = jnp.dot(rows, w[...], preferred_element_type=F32)


def finish_in(n_ring, far, parts, weights):
    width = far.shape[1]
    at = pl.ds(block_start(n_ring // 2, n_ring, width), width)
    return tuple(
        (part[...] + jnp.dot(far[...], w[at, :], preferred_element_type=F32)).astype(BF)
        for part, w in zip(parts, weights)
    )


def attend(query, key, value, ids, base):
    rows, keys = query.shape[0], key.shape[0]
    row = lax.broadcasted_iota(jnp.int32, (rows, keys), 0) + base
    col = lax.broadcasted_iota(jnp.int32, (rows, keys), 1)
    across = jnp.broadcast_to(ids[...], (HD, ids.shape[1]))
    down = jnp.transpose(across)[base : base + rows, :1]
    allowed = (down == ids[:, :keys]) & (col <= row)
    heads = []
    for h in range(query.shape[1] // HD):
        scores = lax.dot_general(
            query[:, h * HD : (h + 1) * HD],
            key,
            (((1,), (1,)), ((), ())),
            preferred_element_type=F32,
        ) * (HD ** -0.5)
        scores = jnp.where(allowed, scores, -jnp.inf)
        expo = jnp.exp(scores - jnp.max(scores, axis=-1, keepdims=True))
        total = jnp.sum(expo, axis=-1, keepdims=True)
        head = jnp.dot(expo.astype(BF), value, preferred_element_type=F32)
        heads.append((head / total).astype(BF))
    return jnp.concatenate(heads, axis=1)


def project_out(mixed, wo, offsets, n_ring, outs):
    width = wo.shape[1] // n_ring
    for out, off in zip(outs, offsets):
        block = wo[:, pl.ds(block_start(off, n_ring, width), width)]
        out[...] = jnp.dot(mixed, block, preferred_element_type=F32).astype(BF)


def first_kernel(n_ring, offsets, far, q, k, v, wq, wk, wv, wo, ids, mixed_out, k_out, v_out, *outs):
    query, key, value = finish_in(n_ring, far, (q, k, v), (wq, wk, wv))
    k_out[...] = key
    v_out[...] = value
    mixed = attend(query, key, value, ids, 0)
    mixed_out[...] = mixed
    project_out(mixed, wo, offsets, n_ring, outs)


def second_kernel(n_ring, offsets, far, q, k, v, k0, v0, wq, wk, wv, wo, ids, mixed_out, *outs):
    query, key, value = finish_in(n_ring, far, (q, k, v), (wq, wk, wv))
    key = jnp.concatenate([k0[...], key], axis=0)
    value = jnp.concatenate([v0[...], value], axis=0)
    mixed = attend(query, key, value, ids, k0.shape[0])
    mixed_out[...] = mixed
    project_out(mixed, wo, offsets, n_ring, outs)


def rest_kernel(n_ring, offsets, mixed, wo, *outs):
    project_out(mixed[...], wo, offsets, n_ring, outs)


def plan_kernel(counts, pick, stay):
    peers = counts.shape[1]
    rows = pick.shape[1]
    me = lax.axis_index("dp")
    start = rows - lax.fori_loop(0, peers, lambda j, n: n + counts[me, j], 0)
    stay[...] = (lax.broadcasted_iota(jnp.int32, stay.shape, 0) < start).astype(F32).astype(BF)
    slot = lax.broadcasted_iota(jnp.int32, (SLOT, rows), 0)
    gap = lax.broadcasted_iota(jnp.int32, (SLOT, rows), 1) - slot

    def step(j, start):
        count = counts[me, j]
        hit = (gap == start) & (slot < count)
        at = pl.multiple_of(j * SLOT, SLOT)
        pick[pl.ds(at, SLOT), :] = hit.astype(F32).astype(BF)
        return start + count

    lax.fori_loop(0, peers, step, start)


def touch_kernel(*refs):
    refs[-1][...] = jnp.zeros(refs[-1].shape, BF)


def finish_kernel(low, pick, stay, own, up, down, *refs):
    *before, leaving, home = refs
    done = own[...].astype(F32) + up[...].astype(F32) + down[...].astype(F32)
    rows = done.shape[0]
    picked = jnp.dot(pick[:, low : low + rows], done.astype(BF), preferred_element_type=F32)
    if before:
        picked = picked + before[0][...].astype(F32)
    leaving[...] = picked.astype(BF)
    kept = jnp.concatenate([stay[low : low + rows, :].astype(F32)] * (done.shape[1] // HD), axis=1)
    home[...] = jnp.where(kept > 0.0, done, 0.0).astype(BF)


def call(kernel, operands, outs, scratch=(), scalars=0, kind=BF):
    vmem = pl.BlockSpec(memory_space=pltpu.VMEM)
    smem = pl.BlockSpec(memory_space=pltpu.SMEM)
    return pl.pallas_call(
        kernel,
        out_shape=[jax.ShapeDtypeStruct(shape, kind) for shape in outs],
        in_specs=[smem] * scalars + [vmem] * (len(operands) - scalars),
        out_specs=[vmem] * len(outs),
        scratch_shapes=scratch,
        compiler_params=pltpu.CompilerParams(vmem_limit_bytes=VMEM_LIMIT),
    )(*operands)


def on_device(hidden, w_query, w_key, w_value, w_out, doc_ids, send_counts):
    peers = lax.axis_size("dp")
    n_ring = lax.axis_size("tensor")
    rows, width = hidden.shape
    kv = w_key.shape[1]
    cut = rows * SPLIT // 16
    up = [(i, (i + 1) % n_ring) for i in range(n_ring)]
    down = [(i, (i - 1) % n_ring) for i in range(n_ring)]

    def send(x, go_up):
        return lax.ppermute(x, "tensor", up if go_up else down)

    def gather(block, far_up):
        shards, a, b = [block], block, block
        for _ in range(n_ring // 2 - 1):
            a, b = send(a, True), send(b, False)
            shards += [a, b]
        return shards + [send(a if far_up else b, far_up)]

    def add(x, y):
        return (x.astype(F32) + y.astype(F32)).astype(BF)

    def reduce(parts, far_up):
        a = send(parts[0], far_up)
        b = None
        for s in range(n_ring // 2 - 1):
            to_up, to_down = parts[1 + 2 * s], parts[2 + 2 * s]
            if s == 0:
                if far_up:
                    a, b = add(to_up, a), to_down
                else:
                    a, b = to_up, add(to_down, a)
            else:
                a, b = add(to_up, a), add(to_down, b)
            a, b = send(a, True), send(b, False)
        return parts[-1], a, b

    w_in = (w_query, w_key, w_value)
    ids = doc_ids[None, :]
    pick, stay = call(plan_kernel, (send_counts,), [(peers * SLOT, rows), (rows, HD)], scalars=1)
    (mark_out,) = call(touch_kernel, (w_out, w_query), [(SLOT, HD)])
    (mark_in,) = call(touch_kernel, (w_key, w_value), [(SLOT, HD)])
    shards_a = gather(hidden[:cut], True)
    shards_b = gather(hidden[cut:], False)
    order = ring_offsets(n_ring)[::-1]
    tile_a, tile_b, kv_a, kv_b = (cut, width), (rows - cut, width), (cut, kv), (rows - cut, kv)
    lead_a, lead_b = (order[0], order[2]), (order[0], order[1])
    late_a = tuple(o for o in order if o not in lead_a)
    late_b = tuple(o for o in order if o not in lead_b)

    pick, stay = call(plan_kernel, (send_counts,), [(peers * SLOT, rows), (rows, HD)], scalars=1)
    (mark_out,) = call(touch_kernel, (w_out, w_query), [(SLOT, HD)])
    (mark_in,) = call(touch_kernel, (w_key, w_value), [(SLOT, HD)])
    shards_a = gather(hidden[:cut], True)
    shards_b = gather(hidden[cut:], False)
    order = ring_offsets(n_ring)[::-1]
    tile_a, tile_b, kv_a, kv_b = (cut, width), (rows - cut, width), (cut, kv), (rows - cut, kv)
    lead_a, lead_b = (order[0], order[2]), (order[0], order[1])
    late_a = tuple(o for o in order if o not in lead_a)
    late_b = tuple(o for o in order if o not in lead_b)

    def early(shards, tile, kv_tile):
        return call(
            functools.partial(early_kernel, n_ring), (*w_in, *shards[:-1]),
            [tile, kv_tile, kv_tile], [pltpu.VMEM((tile[0], n_ring * width), BF)], kind=F32,
        )

    def rest(mixed, tile, offsets):
        return call(
            functools.partial(rest_kernel, n_ring, offsets), (mixed, w_out),
            [tile] * len(offsets),
        )

    early_a = early(shards_a, tile_a, kv_a)
    early_b = early(shards_b, tile_b, kv_b)
    mixed_a, key_a, value_a, *first_a = call(
        functools.partial(first_kernel, n_ring, lead_a),
        (shards_a[-1], *early_a, *w_in, w_out, ids), [tile_a, kv_a, kv_a, tile_a, tile_a],
    )
    mixed_b, *first_b = call(
        functools.partial(second_kernel, n_ring, lead_b),
        (shards_b[-1], *early_b, key_a, value_a, *w_in, w_out, ids), [tile_b] * 3,
    )
    rest_a = rest(mixed_a, tile_a, late_a)
    rest_b = rest(mixed_b, tile_b, late_b)
    parts_a = dict(zip(lead_a + late_a, [*first_a, *rest_a]))
    parts_b = dict(zip(lead_b + late_b, [*first_b, *rest_b]))
    sums_a = reduce([parts_a[o] for o in order], True)
    sums_b = reduce([parts_b[o] for o in order], False)
    slots = (peers * SLOT, width)
    leaving, home_a = call(
        functools.partial(finish_kernel, 0), (pick, stay, *sums_a), [slots, tile_a]
    )
    leaving, home_b = call(
        functools.partial(finish_kernel, cut),
        (pick, stay, *sums_b, leaving, mark_out, mark_in), [slots, tile_b],
    )
    leaving = leaving.reshape(peers, SLOT, width)
    arrived = lax.all_to_all(leaving, "dp", split_axis=0, concat_axis=0, tiled=True)
    return jnp.concatenate([home_a, home_b, arrived.reshape(peers * SLOT, width)], axis=0)


def solution(mesh):
    in_specs = (
        P("dp", "tensor"),
        P(None, "tensor"),
        P(None, "tensor"),
        P(None, "tensor"),
        P("tensor", None),
        P("dp"),
        P(),
    )
    return jax.shard_map(
        on_device, mesh=mesh, in_specs=in_specs, out_specs=P("dp", "tensor"), check_vma=False
    )
```
